1024 devices in a mesh: group: 64 (over z_lo, y), inner: 16 (over x, z_hi, core).
Axes of the slice: x: 4, y: 8, z: 16 (z_hi: 2, z_lo: 8; z = z_hi * 8 + z_lo), core: 2. Of those that a mesh axis runs over, the one named last changes fastest.
Arguments:
- tokens: bfloat16 [393216, 4096], P(('group', 'inner')), may hold values from -6 to 6
- master_weight: float32 [4096, 768], P('inner', 'group'), may hold values from -0.09375 to 0.09375
- first_moment: float32 [4096, 768], P('inner', 'group'), may hold values from -6 to 6
- second_moment: float32 [4096, 768], P('inner', 'group'), may hold values from 0.1 to 10
- gradient: float32 [4096, 768], P('inner', 'group'), may hold values from -6 to 6
- gate_weight: bfloat16 [4096, 2], P('inner'), may hold values from -0.09375 to 0.09375
- input_bias: float32 [1], replicated, may hold values from -3 to -1
- forget_bias: float32 [1], replicated, may hold values from 2 to 5
Outputs:
- new_master: float32 [4096, 768], P('inner', 'group')
- new_first: float32 [4096, 768], P('inner', 'group')
- new_second: float32 [4096, 768], P('inner', 'group')
- hidden: bfloat16 [393216, 256], P(('group', 'inner'))
The draws below stay inside these ranges and needn't reach their ends.
All inputs are finite; a program needn't handle non-finite values.
Results may differ from the reference program's by a relative error of at most 0.012.
Values may be sent and summed in bfloat16 or wider, within the bound.
A program may use at most 32 MiB of HBM per device.

```python
import math
import jax
import jax.numpy as jnp
from jax import lax

D = 4096
QK = 256
V = 256
TOK_DEV = 384
PROJ = 768
TOKENS = 393216


def levels(key, extent, shards, low, top_value):
    gain, own = 1.0, jax.random.fold_in(key, 6)
    for dim, blocks in shards:
        draws = jnp.exp(jax.random.uniform(jax.random.fold_in(own, dim), (blocks,), jnp.float32, low / len(shards), top_value / len(shards)))
        gain = gain * jnp.repeat(draws, extent[dim] // blocks).reshape([-1 if axis == dim else 1 for axis in range(len(extent))])
    return gain


def normal_values(key, dims, deviation, limit, split=(), dtype=jnp.bfloat16):
    values = deviation * jax.random.normal(key, dims, jnp.float32)
    if split:
        values = values * levels(key, dims, split, -0.22, 0.18)
    return jnp.clip(values, -limit, limit).astype(dtype)


def setup_inputs(seed: int = 0) -> dict:
    seeds = jax.random.split(jax.random.key(seed), 9)
    return {
        "tokens": normal_values(seeds[0], (TOKENS, D), 1.0, 6.0, ((0, 1024),)),
        "master_weight": normal_values(seeds[1], (D, PROJ), D ** -0.5, 0.09375, ((0, 16), (1, 64)), jnp.float32),
        "first_moment": normal_values(seeds[2], (D, PROJ), 1.0, 6.0, ((0, 16), (1, 64)), jnp.float32),
        "second_moment": jnp.clip(jnp.exp(math.log(10.0) - 4.6051702 * jax.random.uniform(seeds[3], (D, PROJ), jnp.float32) ** levels(seeds[3], (D, PROJ), ((0, 16), (1, 64)), -0.2, 0.2)), 0.1, 10.0),
        "gradient": normal_values(seeds[4], (D, PROJ), 1.0, 6.0, ((0, 16), (1, 64)), jnp.float32),
        "gate_weight": normal_values(seeds[5], (D, 2), D ** -0.5, 0.09375, ((0, 16),)),
        "input_bias": jnp.clip(jax.random.uniform(seeds[6], (1,), jnp.float32, -3.0, -1.0), -3.0, -1.0),
        "forget_bias": jnp.clip(jax.random.uniform(seeds[7], (1,), jnp.float32, 2.0, 5.0), 2.0, 5.0),
    }


beta_first = 0.9
beta_second = 0.999
learn_rate = 0.001
adam_eps = 1e-08
fix_first = 1.0 - (0.9 ** 10) ** 10
fix_second = 1.0 - (0.999 ** 10) ** 10

def mlstm_head(sequence, projected, gate_pre, input_bias, forget_bias):
    query_rows = projected[:, :QK].astype(jnp.bfloat16)
    key_rows = projected[:, QK:2 * QK].astype(jnp.bfloat16)
    value_rows = projected[:, 2 * QK:].astype(jnp.bfloat16)
    input_gate = gate_pre[:, 0] + input_bias[0]
    forget_log = jax.nn.log_sigmoid(gate_pre[:, 1] + forget_bias[0])
    cumulative = jnp.cumsum(forget_log)
    row_count = sequence.shape[0]
    causal = jnp.arange(row_count)[:, None] >= jnp.arange(row_count)[None, :]
    decay_log = cumulative[:, None] - cumulative[None, :] + input_gate[None, :]
    decay_matrix = jnp.exp(jnp.where(causal, decay_log, -jnp.inf))
    scores = jnp.dot(query_rows, key_rows.T, preferred_element_type=jnp.float32) * QK ** (-0.5)
    weighted = scores * decay_matrix
    normalizer = lax.optimization_barrier(jnp.sum(weighted, axis=1))
    numerator = jnp.dot(weighted.astype(jnp.bfloat16), value_rows, preferred_element_type=jnp.float32)
    return (numerator / jnp.maximum(jnp.abs(normalizer), 1.0)[:, None]).astype(jnp.bfloat16)

def reference(tokens, master_weight, first_moment, second_moment, gradient, gate_weight, input_bias, forget_bias):
    new_first = beta_first * first_moment + (1.0 - beta_first) * gradient
    new_second = beta_second * second_moment + (1.0 - beta_second) * gradient * gradient
    new_master = master_weight - learn_rate * (new_first / fix_first) / (jnp.sqrt(new_second / fix_second) + adam_eps)
    weights = new_master.astype(jnp.bfloat16)

    def mix_sequence(sequence):
        projected = jnp.dot(sequence, weights, preferred_element_type=jnp.float32)
        gate_pre = jnp.dot(sequence, gate_weight, preferred_element_type=jnp.float32)
        return mlstm_head(sequence, projected, gate_pre, input_bias, forget_bias)
    hidden = lax.map(mix_sequence, tokens.reshape(-1, TOK_DEV, D))
    return (new_master, new_first, new_second, hidden.reshape(-1, V))
```

```python
import functools

import jax
import jax.numpy as jnp
from jax import lax
from jax.experimental import pallas as pl
from jax.experimental.pallas import tpu as pltpu
from jax.sharding import PartitionSpec as P

MESH = pl.DeviceIdType.MESH

QK = 256
NX, NY, NZL, NZH = 4, 8, 8, 2
NZ = NZL * NZH
TOK = 384
CHUNK = 256
HALF = 128
COLS = 12
BLOCKS = NX * NZH
ROWS_A = NY * NZL * 8
ROWS_B = NZL * NY * 4
ROWS_G = 16
ROWS = ROWS_A + ROWS_B + ROWS_G

VMEM_ALL = 67_043_328

beta_first = 0.9
beta_second = 0.999
learn_rate = 0.001
adam_eps = 1e-08
fix_first = 1.0 - (0.9**10) ** 10
fix_second = 1.0 - (0.999**10) ** 10

NT = (((1,), (1,)), ((), ()))


def adam(master, first, second, gradient):
    new_first = beta_first * first + (1.0 - beta_first) * gradient
    new_second = beta_second * second + (1.0 - beta_second) * gradient * gradient
    new_master = master - learn_rate * (new_first / fix_first) / (
        jnp.sqrt(new_second / fix_second) + adam_eps
    )
    return new_master, new_first, new_second


class Sems:
    def __init__(self, send, recv):
        self.send, self.recv, self.used, self.sent = send, recv, 0, []

    def copy(self, src, dst, device):
        k = self.used
        self.used += 1
        return pltpu.make_async_remote_copy(
            src_ref=src,
            dst_ref=dst,
            send_sem=self.send.at[k],
            recv_sem=self.recv.at[k],
            device_id=device,
            device_id_type=MESH,
        )


def gather_kernel(
    tokens,
    master,
    first,
    second,
    gradient,
    gate,
    out,
    gate_out,
    state,
    gate_in,
    x,
    pa,
    y1,
    pb,
    pg,
    wt,
    acc,
    part_out,
    part_in,
    send_sem,
    recv_sem,
    local_sem,
):
    group, inner = lax.axis_index("group"), lax.axis_index("inner")
    zl, y = group // NY, group % NY
    xc, zh, core = inner // 4, (inner // 2) % 2, inner % 2
    z = zh * NZL + zl
    sems = Sems(send_sem, recv_sem)
    started = []

    def device(x_=xc, y_=y, z_=z, core_=core):
        return ((z_ % NZL) * NY + y_, x_ * 4 + (z_ // NZL) * 2 + core_)

    def at_x(r):
        return device(x_=(xc + r + NX) % NX)

    def at_y(r):
        return device(y_=(y + r + NY) % NY)

    def at_z(r):
        return device(z_=(z + r + NZ) % NZ)

    other = device(core_=1 - core)

    def go(src, dst, dev):
        c = sems.copy(src, dst, dev)
        c.start()
        started.append(c)
        return c

    loads = [
        pltpu.make_async_copy(src, dst, local_sem.at[BLOCKS + k])
        for k, (src, dst) in enumerate(
            [(ref, state.at[k]) for k, ref in enumerate((master, first, second, gradient))]
            + [(gate, gate_in)]
        )
    ]
    for c in loads:
        c.start()

    local = []
    for m in range(BLOCKS):
        c = pltpu.make_async_copy(
            tokens.at[:, pl.ds(pl.multiple_of((2 * m + core) * CHUNK, CHUNK), CHUNK)],
            x.at[pl.ds(0, TOK), pl.ds(m * CHUNK, CHUNK)],
            local_sem.at[m],
        )
        c.start()
        local.append(c)

    barrier = pltpu.get_barrier_semaphore()
    peers = (
        [at_z(r) for r in range(1, NZ)]
        + [at_y(r) for r in range(1, NY)]
        + [at_x(r) for r in range(1, NX)]
        + [other]
    )
    for peer in peers:
        pl.semaphore_signal(barrier, inc=1, device_id=peer, device_id_type=MESH)

    for c in loads:
        c.wait()
    new_master, _, _ = adam(state[0], state[1], state[2], state[3])
    pa[0, xc, zh, y, zl] = new_master[0:8, 0:HALF].astype(jnp.bfloat16)
    pa[1, xc, zh, y, zl] = new_master[0:8, HALF:].astype(jnp.bfloat16)
    y1[y] = jnp.concatenate([new_master[8:12, 0:HALF], new_master[8:12, HALF:]], axis=0).astype(
        jnp.bfloat16
    )
    gate_rows = jnp.concatenate(
        [gate_in[...].astype(jnp.float32), jnp.zeros((ROWS_G - 2, CHUNK), jnp.float32)], axis=0
    ).astype(jnp.bfloat16)
    pg[xc, zh, 0] = gate_rows[:, 0:HALF]
    pg[xc, zh, 1] = gate_rows[:, HALF:]

    pl.semaphore_wait(barrier, len(peers))

    b_y = [go(y1.at[y], y1.at[y], at_y(r)) for r in range(1, NY)]
    a_z = [
        go(pa.at[:, xc, zh, y, zl], pa.at[:, xc, zh, y, zl], at_z(r))
        for r in (8, 7, 9, 6, 10, 5, 11, 4, 12, 3, 13, 2, 14, 1, 15)
    ]
    g_z = go(pg.at[xc, zh], pg.at[xc, zh], at_z(NZL))
    given = [
        go(
            tokens.at[:, pl.ds(pl.multiple_of((2 * m + 1 - core) * CHUNK, CHUNK), CHUNK)],
            x.at[pl.ds(TOK, TOK), pl.ds(m * CHUNK, CHUNK)],
            other,
        )
        for m in range(BLOCKS)
    ]

    for c in b_y:
        c.wait_recv()
    upper = lax.broadcasted_iota(jnp.int32, (8, HALF), 0) < 4
    low, high = [], []
    for a in range(NY // 2):
        even = y1[2 * a].astype(jnp.float32)
        odd = y1[2 * a + 1].astype(jnp.float32)
        low.append(jnp.where(upper, even, pltpu.roll(odd, 4, 0)))
        high.append(jnp.where(upper, pltpu.roll(even, 4, 0), odd))
    pb[xc, zh, 0, zl] = jnp.concatenate(low, axis=0).astype(jnp.bfloat16)
    pb[xc, zh, 1, zl] = jnp.concatenate(high, axis=0).astype(jnp.bfloat16)
    b_x = [
        go(pb.at[xc, zh, :, zl], pb.at[xc, zh, :, zl], at_x(r)) for r in (2, 1, 3)
    ]
    for c in b_x:
        c.wait_recv()

    def ring(count, chunks, region, coord, neighbour):
        half = count // 2
        copies = {}

        def send(sign, step):
            parts = range(chunks)
            if step == half:
                parts = range(chunks // 2) if sign > 0 else range(chunks // 2, chunks)
            block = (coord - sign * (step - 1) + count) % count
            for k in parts:
                copies[sign, step, k] = go(region(block, k), region(block, k), neighbour(sign))

        def advance(step):
            for k in range(chunks):
                for sign in (1, -1):
                    if (sign, step, k) in copies:
                        copies[sign, step, k].wait_recv()
                        last = step + 1 == half
                        if step < half and (not last or (k < chunks // 2) == (sign > 0)):
                            block = (coord - sign * step + count) % count
                            copies[sign, step + 1, k] = go(
                                region(block, k), region(block, k), neighbour(sign)
                            )

        send(1, 1)
        send(-1, 1)
        return advance

    z_ring = ring(
        NZ,
        2,
        lambda b, k: pb.at[pl.ds(2 * k, 2), b // NZL, :, b % NZL],
        z,
        at_z,
    )

    for c in a_z:
        c.wait_recv()
    a_x = [go(pa.at[0, xc, :, y], pa.at[0, xc, :, y], at_x(r)) for r in (2, 1, 3)]
    a_y = [go(pa.at[1, xc, :, y], pa.at[1, xc, :, y], at_y(r)) for r in (4, 3, 5, 2, 6, 1, 7)]
    g_z.wait_recv()
    g_x = [go(pg.at[xc], pg.at[xc], at_x(r)) for r in (2, 1, 3)]

    z_ring(1)
    for c in a_x:
        c.wait_recv()
    y_ring = ring(NY, 4, lambda b, k: pa.at[0, k, :, b], y, at_y)
    z_ring(2)
    y_ring(1)
    for c in a_y:
        c.wait_recv()
    x_ring = ring(NX, 4, lambda b, k: pa.at[1, b, k // 2, pl.ds(4 * (k % 2), 4)], xc, at_x)
    z_ring(3)
    y_ring(2)
    z_ring(4)
    x_ring(1)
    y_ring(3)
    z_ring(5)
    y_ring(4)
    z_ring(6)
    x_ring(2)
    z_ring(7)
    z_ring(8)
    for c in g_x:
        c.wait_recv()
    for c in local:
        c.wait()
    for c in given:
        c.wait_recv()

    for m in range(BLOCKS):
        mx, mz = m // 2, m % 2
        for kh in range(2):
            lanes = pl.ds(m * CHUNK + kh * HALF, HALF)
            wt[0:ROWS_A, lanes] = pa[kh, mx, mz].reshape(ROWS_A, HALF)
            wt[ROWS_A : ROWS_A + ROWS_B, lanes] = pb[mx, mz, kh].reshape(ROWS_B, HALF)
            wt[ROWS_A + ROWS_B :, lanes] = pg[mx, mz, kh]

    summed = []
    for lo, hi in ((512, 784), (0, 256), (256, 512)):
        res = lax.dot_general(wt[lo:hi], x[...], NT, preferred_element_type=jnp.float32)
        acc[lo:hi] = res[:, :TOK]
        part_out[lo:hi] = res[:, TOK:]
        summed.append(go(part_out.at[pl.ds(lo, hi - lo)], part_in.at[pl.ds(lo, hi - lo)], other))
    for c in summed:
        c.wait_recv()

    gate_out[...] = acc[768:776] + part_in[768:776]
    first4 = lax.broadcasted_iota(jnp.int32, (8, TOK), 0) < 4
    for l in range(NZL):
        rows = []
        for a in range(NY // 2):
            even = ((2 * a) * NZL + l) * 8
            odd = ((2 * a + 1) * NZL + l) * 8
            mixed = ROWS_A + (l * NY + 2 * a) * 4
            t0, a1, b = (
                acc[r : r + 8] + part_in[r : r + 8] for r in (even, odd, mixed)
            )
            turned = pltpu.roll(a1, 4, 0)
            rows += [t0, jnp.where(first4, b, turned), jnp.where(first4, turned, b)]
        out[l * 96 : l * 96 + 96] = jnp.concatenate(rows, axis=0).astype(jnp.bfloat16)

    for c in started:
        c.wait_send()


def head_kernel(
    projected,
    gates,
    input_bias,
    forget_bias,
    master,
    first,
    second,
    gradient,
    new_master,
    new_first,
    new_second,
    hidden,
    state,
    updated,
    sems,
):
    loads = [
        pltpu.make_async_copy(ref, state.at[k], sems.at[k])
        for k, ref in enumerate((master, first, second, gradient))
    ]
    for c in loads:
        c.start()
    for c in loads:
        c.wait()
    updated[0], updated[1], updated[2] = adam(state[0], state[1], state[2], state[3])
    stores = [
        pltpu.make_async_copy(updated.at[k], ref, sems.at[4 + k])
        for k, ref in enumerate((new_master, new_first, new_second))
    ]
    for c in stores:
        c.start()
    pre = gates[...]
    input_gate = pre[0:1] + input_bias[0]
    forget = pre[1:2] + forget_bias[0]
    forget_log = jnp.minimum(forget, 0.0) - jnp.log1p(jnp.exp(-jnp.abs(forget)))
    t = lax.broadcasted_iota(jnp.int32, (TOK, TOK), 0)
    s = lax.broadcasted_iota(jnp.int32, (TOK, TOK), 1)
    causal = t >= s
    column = jnp.sum(jnp.where(causal, forget_log, 0.0), axis=1, keepdims=True)
    lane = lax.broadcasted_iota(jnp.int32, (8, TOK), 1)
    scan = jnp.broadcast_to(forget_log, (8, TOK))
    step = 1
    while step < TOK:
        scan = scan + jnp.where(lane >= step, pltpu.roll(scan, step, 1), 0.0)
        step *= 2
    row = scan[0:1]
    decay = jnp.exp(jnp.where(causal, column - row + input_gate, -jnp.inf))
    query = projected[0:QK].T
    scores = jnp.dot(query, projected[QK : 2 * QK], preferred_element_type=jnp.float32)
    weighted = scores * QK ** (-0.5) * decay
    normalizer = jnp.sum(weighted, axis=1, keepdims=True)
    numerator = lax.dot_general(
        weighted.astype(jnp.bfloat16),
        projected[2 * QK :],
        NT,
        preferred_element_type=jnp.float32,
    )
    hidden[...] = (numerator / jnp.maximum(jnp.abs(normalizer), 1.0)).astype(jnp.bfloat16)
    for c in stores:
        c.wait()


def on_device(
    tokens,
    master_weight,
    first_moment,
    second_moment,
    gradient,
    gate_weight,
    input_bias,
    forget_bias,
):
    state = [a.T for a in (master_weight, first_moment, second_moment, gradient)]
    vmem = pl.BlockSpec(memory_space=pltpu.VMEM)
    smem = pl.BlockSpec(memory_space=pltpu.SMEM)
    hbm = pl.BlockSpec(memory_space=pltpu.HBM)
    bf16, f32 = jnp.bfloat16, jnp.float32
    copies = 160
    projected, gates = pl.pallas_call(
        gather_kernel,
        out_shape=(
            jax.ShapeDtypeStruct((3 * QK, TOK), bf16),
            jax.ShapeDtypeStruct((8, TOK), f32),
        ),
        in_specs=[hbm] * 6,
        out_specs=(vmem, vmem),
        scratch_shapes=[
            pltpu.VMEM((4, COLS, CHUNK), f32),
            pltpu.VMEM((2, CHUNK), bf16),
            pltpu.VMEM((2 * TOK, BLOCKS * CHUNK), bf16),
            pltpu.VMEM((2, NX, NZH, NY, NZL, 8, HALF), bf16),
            pltpu.VMEM((NY, 8, HALF), bf16),
            pltpu.VMEM((NX, NZH, 2, NZL, 32, HALF), bf16),
            pltpu.VMEM((NX, NZH, 2, ROWS_G, HALF), bf16),
            pltpu.VMEM((ROWS, BLOCKS * CHUNK), bf16),
            pltpu.VMEM((ROWS, TOK), f32),
            pltpu.VMEM((ROWS, TOK), f32),
            pltpu.VMEM((ROWS, TOK), f32),
            pltpu.SemaphoreType.DMA((copies,)),
            pltpu.SemaphoreType.DMA((copies,)),
            pltpu.SemaphoreType.DMA((BLOCKS + 5,)),
        ],
        compiler_params=pltpu.CompilerParams(
            collective_id=0, has_side_effects=True, vmem_limit_bytes=VMEM_ALL
        ),
        name="gather_project",
    )(tokens, *state, gate_weight.T)
    new_master, new_first, new_second, hidden = pl.pallas_call(
        head_kernel,
        out_shape=tuple(jax.ShapeDtypeStruct((COLS, CHUNK), f32) for _ in range(3))
        + (jax.ShapeDtypeStruct((TOK, QK), bf16),),
        in_specs=[vmem, vmem, smem, smem] + [hbm] * 4,
        out_specs=(hbm,) * 3 + (vmem,),
        scratch_shapes=[
            pltpu.VMEM((4, COLS, CHUNK), f32),
            pltpu.VMEM((3, COLS, CHUNK), f32),
            pltpu.SemaphoreType.DMA((7,)),
        ],
        compiler_params=pltpu.CompilerParams(vmem_limit_bytes=VMEM_ALL),
        name="head",
    )(projected, gates, input_bias, forget_bias, *state)
    return new_master.T, new_first.T, new_second.T, hidden


def solution(mesh):
    placed = (
        P(("group", "inner"), None),
        P("inner", "group"),
        P("inner", "group"),
        P("inner", "group"),
        P("inner", "group"),
        P("inner", None),
        P(),
        P(),
    )
    return jax.shard_map(
        on_device,
        mesh=mesh,
        in_specs=placed,
        out_specs=(
            P("inner", "group"),
            P("inner", "group"),
            P("inner", "group"),
            P(("group", "inner"), None),
        ),
        check_vma=False,
    )
```

```python
import functools

import jax
import jax.numpy as jnp
from jax import lax
from jax.experimental import pallas as pl
from jax.experimental.pallas import tpu as pltpu
from jax.sharding import PartitionSpec as P

MESH = pl.DeviceIdType.MESH

QK = 256
NX, NY, NZL, NZH = 4, 8, 8, 2
NZ = NZL * NZH
REACH = 4
TOK = 384
CHUNK = 256
HALF = 128
COLS = 12
BLOCKS = NX * NZH * 2
ROWS_A = NY * NZL * 8
ROWS_B = NZL * NY * 4
ROWS_G = 16

VMEM_ALL = 67_043_328

beta_first = 0.9
beta_second = 0.999
learn_rate = 0.001
adam_eps = 1e-08
fix_first = 1.0 - (0.9**10) ** 10
fix_second = 1.0 - (0.999**10) ** 10

NT = (((1,), (1,)), ((), ()))


def adam(master, first, second, gradient):
    new_first = beta_first * first + (1.0 - beta_first) * gradient
    new_second = beta_second * second + (1.0 - beta_second) * gradient * gradient
    new_master = master - learn_rate * (new_first / fix_first) / (
        jnp.sqrt(new_second / fix_second) + adam_eps
    )
    return new_master, new_first, new_second


def gather_kernel(
    tokens,
    master,
    first,
    second,
    gradient,
    gate,
    out,
    gate_out,
    state,
    gate_in,
    x,
    pa,
    y1,
    pb,
    pg,
    gate_far,
    wt,
    a_rows,
    b_rows,
    g_rows,
    a_give,
    b_give,
    g_give,
    send_sem,
    recv_sem,
    local_sem,
):
    group, inner = lax.axis_index("group"), lax.axis_index("inner")
    zl, y = group // NY, group % NY
    xc, zh, core = inner // 4, (inner // 2) % 2, inner % 2
    z = zh * NZL + zl
    here = (xc, zh, y, zl)

    def device(x_=xc, y_=y, z_=z, core_=core):
        return ((z_ % NZL) * NY + y_, x_ * 4 + (z_ // NZL) * 2 + core_)

    def at_x(r):
        return device(x_=(xc + r + NX) % NX)

    def at_y(r):
        return device(y_=(y + r + NY) % NY)

    def at_z(r):
        return device(z_=(z + r + NZ) % NZ)

    other = device(core_=1 - core)

    loads = [
        pltpu.make_async_copy(src, dst, local_sem.at[1 + k])
        for k, (src, dst) in enumerate(
            [(ref, state.at[k]) for k, ref in enumerate((master, first, second, gradient))]
            + [(gate, gate_in)]
        )
    ]
    for c in loads:
        c.start()
    own_tokens = pltpu.make_async_copy(tokens, x.at[pl.ds(0, TOK)], local_sem.at[0])
    own_tokens.start()

    barrier = pltpu.get_barrier_semaphore()
    peers = (
        [at_z(sign * r) for r in range(1, REACH + 1) for sign in (1, -1)]
        + [at_y(r) for r in range(1, NY)]
        + [at_x(r) for r in range(1, NX)]
        + [other]
    )
    for peer in peers:
        pl.semaphore_signal(barrier, inc=1, device_id=peer, device_id_type=MESH)

    for c in loads:
        c.wait()
    new_master, _, _ = adam(state[0], state[1], state[2], state[3])
    pa[(0, *here, core)] = new_master[0:8, 0:HALF].astype(jnp.bfloat16)
    pa[(1, *here, core)] = new_master[0:8, HALF:].astype(jnp.bfloat16)
    y1[y, core] = jnp.concatenate(
        [new_master[8:12, 0:HALF], new_master[8:12, HALF:]], axis=0
    ).astype(jnp.bfloat16)
    gate_rows = jnp.concatenate(
        [gate_in[...].astype(jnp.float32), jnp.zeros((ROWS_G - 2, CHUNK), jnp.float32)], axis=0
    ).astype(jnp.bfloat16)
    pg[xc, core, 0] = gate_rows[:, 0:HALF]
    pg[xc, core, 1] = gate_rows[:, HALF:]

    pl.semaphore_wait(barrier, len(peers))

    a_tiles = (pa.at[(slice(0, 2), *here, 1)],) * 2
    b_tile = (y1.at[y, 0],) * 2
    g_tile = (pg.at[xc, 0],) * 2
    all_tokens = (tokens, x.at[pl.ds(TOK, TOK)])
    a_parts = [
        (a_give.at[pl.ds(k * 32, 32)], a_rows.at[pl.ds(k * 32, 32)]) for k in range(2)
    ]
    b_part, g_part = (b_give, b_rows), (g_give, g_rows)
    across = [a_tiles, b_tile, g_tile, all_tokens, *a_parts, b_part, g_part]

    def cross(pair):
        k = [p is pair for p in across].index(True)
        return pltpu.make_async_remote_copy(
            src_ref=pair[0],
            dst_ref=pair[1],
            send_sem=send_sem.at[k],
            recv_sem=recv_sem.at[k],
            device_id=other,
            device_id_type=MESH,
        )

    class Plan:
        def __init__(self):
            self.used, self.started = len(across), []

        def go(self, src, dev, dst=None):
            k = self.used
            self.used += 1
            c = pltpu.make_async_remote_copy(
                src_ref=src,
                dst_ref=src if dst is None else dst,
                send_sem=send_sem.at[k],
                recv_sem=recv_sem.at[k],
                device_id=dev,
                device_id_type=MESH,
            )
            c.start()
            self.started.append(c)
            return c

        def give(self, pair):
            c = cross(pair)
            c.start()
            self.started.append(c)

    def ring(go, count, chunks, region, coord, neighbour):
        half = count // 2
        copies = {}

        def begin(parts):
            for k in parts:
                for sign in (1, -1):
                    copies[sign, 1, k] = go(region(coord, k), neighbour(sign))

        def advance(step, k):
            for sign in (1, -1):
                if (sign, step, k) in copies:
                    copies[sign, step, k].wait_recv()
                    last = step + 1 == half
                    if step < half and (not last or (k < chunks // 2) == (sign > 0)):
                        block = (coord - sign * step + count) % count
                        copies[sign, step + 1, k] = go(region(block, k), neighbour(sign))

        return begin, advance

    def run(events):
        for _, event in sorted(events, key=lambda e: e[0]):
            event()

    @pl.when(core == 0)
    def _():
        plan = Plan()
        go = plan.go
        plan.give(b_tile)
        plan.give(g_tile)
        cross(a_tiles).wait_recv()

        def tile(slots, block):
            return pa.at[slots, xc, block // NZL, y, block % NZL]

        both = slice(0, 2)
        along_x, along_y = [], []

        def spread_x(block):
            along_x.extend(go(tile(0, block), at_x(r)) for r in (2, 1, 3))

        def spread_y(block):
            along_y.extend(go(tile(1, block), at_y(r)) for r in (4, 3, 5, 2, 6, 1, 7))

        a_z = {}
        for r in range(REACH, 0, -1):
            for sign in (1, -1):
                a_z[sign, r] = go(tile(both, z), at_z(sign * r))
        spread_y(z)
        spread_x(z)
        plan.give(all_tokens)
        for r in range(1, 2 * REACH + 1):
            for sign in (1, -1):
                block = (z - sign * r + NZ) % NZ
                a_z[sign, r].wait_recv()
                if r <= REACH:
                    slots = both if r < REACH else slice(0, 1) if sign > 0 else slice(1, 2)
                    a_z[sign, REACH + r] = go(tile(slots, block), at_z(sign * REACH))
                if r < 2 * REACH or sign < 0:
                    spread_y(block)
                if r < 2 * REACH or sign > 0:
                    spread_x(block)

        y_begin, y_step = ring(go, NY, NX, lambda b, k: pa.at[0, k, :, b], y, at_y)
        x_begin, x_step = ring(
            go, NX, 8, lambda b, k: pa.at[1, b, k // 4, pl.ds(2 * (k % 4), 2)], xc, at_x
        )

        def start(copies, begin, chunks):
            for c in copies:
                c.wait_recv()
            begin(range(chunks))

        events = [
            (13.6, lambda: start(along_x, y_begin, NX)),
            (15.6, lambda: start(along_y, x_begin, 8)),
        ]
        for step in range(1, NY // 2 + 1):
            for k in range(NX):
                events.append((16.3 + 2.8 * (step - 1) + 0.7 * k, functools.partial(y_step, step, k)))
        for step in range(1, NX // 2 + 1):
            for k in range(8):
                when = 18.5 + 5.6 * (step - 1) + 0.7 * (k if step == 1 else k % 4)
                events.append((when, functools.partial(x_step, step, k)))
        run(events)

        own_tokens.wait()
        cross(all_tokens).wait_recv()
        for block in range(BLOCKS):
            mx, mz, parity = block // 4, (block // 2) % 2, block % 2
            for kh in range(2):
                lanes = pl.ds(block * CHUNK + kh * HALF, HALF)
                wt[:, lanes] = pa[kh, mx, mz, :, :, parity].reshape(ROWS_A, HALF)
        for k in range(2):
            res = lax.dot_general(
                wt[k * 256 : (k + 1) * 256], x[...], NT, preferred_element_type=jnp.float32
            )
            res = res.reshape(32, 8, 2 * TOK).astype(jnp.bfloat16)
            a_give[k * 32 : (k + 1) * 32] = res[:, :, TOK:]
            plan.give(a_parts[k])
            a_rows[k * 32 : (k + 1) * 32] = res[:, :, :TOK]
        cross(g_part).wait_recv()
        cross(b_part).wait_recv()
        for c in plan.started:
            c.wait_send()

    @pl.when(core == 1)
    def _():
        plan = Plan()
        go = plan.go
        plan.give(a_tiles)
        cross(b_tile).wait_recv()
        b_y = [go(y1.at[y], at_y(r)) for r in (4, 3, 5, 2, 6, 1, 7)]
        cross(g_tile).wait_recv()
        g_x = [go(pg.at[xc], at_x(r)) for r in (2, 1, 3)]
        plan.give(all_tokens)
        for c in b_y:
            c.wait_recv()
        upper = lax.broadcasted_iota(jnp.int32, (8, HALF), 0) < 4
        for parity in range(2):
            low, high = [], []
            for a in range(NY // 2):
                even = y1[2 * a, parity].astype(jnp.float32)
                odd = y1[2 * a + 1, parity].astype(jnp.float32)
                low.append(jnp.where(upper, even, pltpu.roll(odd, 4, 0)))
                high.append(jnp.where(upper, pltpu.roll(even, 4, 0), odd))
            pb[xc, zh, zl, parity, 0] = jnp.concatenate(low, axis=0).astype(jnp.bfloat16)
            pb[xc, zh, zl, parity, 1] = jnp.concatenate(high, axis=0).astype(jnp.bfloat16)
        for c in g_x:
            c.wait_recv()
        b_x = [go(pb.at[xc, zh, zl], at_x(r)) for r in (1, 3, 2)]
        begin, step_of = ring(
            go, NZ, NX, lambda b, k: pb.at[(xc + k) % NX, b // NZL, b % NZL], z, at_z
        )
        begin((0,))
        g_z = [
            go(pg, at_z(sign * REACH), gate_far.at[k]) for k, sign in ((0, 1), (1, -1))
        ]

        def start(c, k):
            c.wait_recv()
            begin((k,))

        events = [
            (2.5, lambda: start(b_x[0], 3)),
            (2.6, lambda: start(b_x[1], 1)),
            (3.6, lambda: start(b_x[2], 2)),
        ]
        for step in range(1, NZ // 2 + 1):
            for k, late in ((0, 0.3), (1, 2.9), (3, 3.2), (2, 4.2)):
                events.append((late + 2.4 * step, functools.partial(step_of, step, k)))
        run(events)

        for c in g_z:
            c.wait_recv()
        for block in range(BLOCKS):
            mx, mz, parity = block // 4, (block // 2) % 2, block % 2
            for kh in range(2):
                lanes = pl.ds(block * CHUNK + kh * HALF, HALF)
                wt[0:ROWS_B, lanes] = pb[mx, mz, :, parity, kh].reshape(ROWS_B, HALF)
        for mx in range(NX):
            for parity in range(2):
                for kh in range(2):
                    near = (4 * mx + 2 * zh + parity) * CHUNK + kh * HALF
                    far = (4 * mx + 2 * (1 - zh) + parity) * CHUNK + kh * HALF
                    rows = pl.ds(ROWS_B, ROWS_G)
                    wt[rows, pl.ds(pl.multiple_of(near, HALF), HALF)] = pg[mx, parity, kh]
                    wt[rows, pl.ds(pl.multiple_of(far, HALF), HALF)] = gate_far[
                        zl // REACH, mx, parity, kh
                    ]
        own_tokens.wait()
        cross(all_tokens).wait_recv()
        res = lax.dot_general(
            wt[0 : ROWS_B + ROWS_G], x[...], NT, preferred_element_type=jnp.float32
        )
        g_rows[...] = res[ROWS_B:, :TOK]
        g_give[...] = res[ROWS_B:, TOK:]
        plan.give(g_part)
        res = res[:ROWS_B].reshape(32, 8, 2 * TOK).astype(jnp.bfloat16)
        b_give[...] = res[:, :, TOK:]
        plan.give(b_part)
        b_rows[...] = res[:, :, :TOK]
        for pair in a_parts:
            cross(pair).wait_recv()
        for c in plan.started:
            c.wait_send()

    gate_out[...] = g_rows[0:8]
    first4 = lax.broadcasted_iota(jnp.int32, (8, TOK), 0) < 4
    for l in range(NZL):
        rows = []
        for a in range(NY // 2):
            t0 = a_rows[2 * a * NZL + l].astype(jnp.float32)
            a1 = a_rows[(2 * a + 1) * NZL + l].astype(jnp.float32)
            b = b_rows[l * (NY // 2) + a].astype(jnp.float32)
            turned = pltpu.roll(a1, 4, 0)
            rows += [t0, jnp.where(first4, b, turned), jnp.where(first4, turned, b)]
        out[l * 96 : l * 96 + 96] = jnp.concatenate(rows, axis=0).astype(jnp.bfloat16)


def head_kernel(
    projected,
    gates,
    input_bias,
    forget_bias,
    master,
    first,
    second,
    gradient,
    new_master,
    new_first,
    new_second,
    hidden,
    state,
    updated,
    sems,
):
    loads = [
        pltpu.make_async_copy(ref, state.at[k], sems.at[k])
        for k, ref in enumerate((master, first, second, gradient))
    ]
    for c in loads:
        c.start()
    for c in loads:
        c.wait()
    updated[0], updated[1], updated[2] = adam(state[0], state[1], state[2], state[3])
    stores = [
        pltpu.make_async_copy(updated.at[k], ref, sems.at[4 + k])
        for k, ref in enumerate((new_master, new_first, new_second))
    ]
    for c in stores:
        c.start()
    pre = gates[...]
    input_gate = pre[0:1] + input_bias[0]
    forget = pre[1:2] + forget_bias[0]
    forget_log = jnp.minimum(forget, 0.0) - jnp.log1p(jnp.exp(-jnp.abs(forget)))
    t = lax.broadcasted_iota(jnp.int32, (TOK, TOK), 0)
    s = lax.broadcasted_iota(jnp.int32, (TOK, TOK), 1)
    causal = t >= s
    column = jnp.sum(jnp.where(causal, forget_log, 0.0), axis=1, keepdims=True)
    lane = lax.broadcasted_iota(jnp.int32, (8, TOK), 1)
    scan = jnp.broadcast_to(forget_log, (8, TOK))
    step = 1
    while step < TOK:
        scan = scan + jnp.where(lane >= step, pltpu.roll(scan, step, 1), 0.0)
        step *= 2
    row = scan[0:1]
    decay = jnp.exp(jnp.where(causal, column - row + input_gate, -jnp.inf))
    query = projected[0:QK].T
    scores = jnp.dot(query, projected[QK : 2 * QK], preferred_element_type=jnp.float32)
    weighted = scores * QK ** (-0.5) * decay
    normalizer = jnp.sum(weighted, axis=1, keepdims=True)
    numerator = lax.dot_general(
        weighted.astype(jnp.bfloat16),
        projected[2 * QK :],
        NT,
        preferred_element_type=jnp.float32,
    )
    hidden[...] = (numerator / jnp.maximum(jnp.abs(normalizer), 1.0)).astype(jnp.bfloat16)
    for c in stores:
        c.wait()


def on_device(
    tokens,
    master_weight,
    first_moment,
    second_moment,
    gradient,
    gate_weight,
    input_bias,
    forget_bias,
):
    state = [a.T for a in (master_weight, first_moment, second_moment, gradient)]
    vmem = pl.BlockSpec(memory_space=pltpu.VMEM)
    smem = pl.BlockSpec(memory_space=pltpu.SMEM)
    hbm = pl.BlockSpec(memory_space=pltpu.HBM)
    bf16, f32 = jnp.bfloat16, jnp.float32
    copies = 256
    projected, gates = pl.pallas_call(
        gather_kernel,
        out_shape=(
            jax.ShapeDtypeStruct((3 * QK, TOK), bf16),
            jax.ShapeDtypeStruct((8, TOK), f32),
        ),
        in_specs=[hbm] * 6,
        out_specs=(vmem, vmem),
        scratch_shapes=[
            pltpu.VMEM((4, COLS, CHUNK), f32),
            pltpu.VMEM((2, CHUNK), bf16),
            pltpu.VMEM((2 * TOK, BLOCKS * CHUNK), bf16),
            pltpu.VMEM((2, NX, NZH, NY, NZL, 2, 8, HALF), bf16),
            pltpu.VMEM((NY, 2, 8, HALF), bf16),
            pltpu.VMEM((NX, NZH, NZL, 2, 2, 32, HALF), bf16),
            pltpu.VMEM((NX, 2, 2, ROWS_G, HALF), bf16),
            pltpu.VMEM((2, NX, 2, 2, ROWS_G, HALF), bf16),
            pltpu.VMEM((ROWS_A, BLOCKS * CHUNK), bf16),
            pltpu.VMEM((64, 8, TOK), bf16),
            pltpu.VMEM((32, 8, TOK), bf16),
            pltpu.VMEM((ROWS_G, TOK), f32),
            pltpu.VMEM((64, 8, TOK), bf16),
            pltpu.VMEM((32, 8, TOK), bf16),
            pltpu.VMEM((ROWS_G, TOK), f32),
            pltpu.SemaphoreType.DMA((copies,)),
            pltpu.SemaphoreType.DMA((copies,)),
            pltpu.SemaphoreType.DMA((6,)),
        ],
        compiler_params=pltpu.CompilerParams(
            collective_id=0, has_side_effects=True, vmem_limit_bytes=VMEM_ALL
        ),
        name="gather_project",
    )(tokens, *state, gate_weight.T)
    new_master, new_first, new_second, hidden = pl.pallas_call(
        head_kernel,
        out_shape=tuple(jax.ShapeDtypeStruct((COLS, CHUNK), f32) for _ in range(3))
        + (jax.ShapeDtypeStruct((TOK, QK), bf16),),
        in_specs=[vmem, vmem, smem, smem] + [hbm] * 4,
        out_specs=(hbm,) * 3 + (vmem,),
        scratch_shapes=[
            pltpu.VMEM((4, COLS, CHUNK), f32),
            pltpu.VMEM((3, COLS, CHUNK), f32),
            pltpu.SemaphoreType.DMA((7,)),
        ],
        compiler_params=pltpu.CompilerParams(vmem_limit_bytes=VMEM_ALL),
        name="head",
    )(projected, gates, input_bias, forget_bias, *state)
    return new_master.T, new_first.T, new_second.T, hidden


def solution(mesh):
    placed = (
        P(("group", "inner"), None),
        P("inner", "group"),
        P("inner", "group"),
        P("inner", "group"),
        P("inner", "group"),
        P("inner", None),
        P(),
        P(),
    )
    return jax.shard_map(
        on_device,
        mesh=mesh,
        in_specs=placed,
        out_specs=(
            P("inner", "group"),
            P("inner", "group"),
            P("inner", "group"),
            P(("group", "inner"), None),
        ),
        check_vma=False,
    )
```

```python
import functools

import jax
import jax.numpy as jnp
from jax import lax
from jax.experimental import pallas as pl
from jax.experimental.pallas import tpu as pltpu
from jax.sharding import PartitionSpec as P

MESH = pl.DeviceIdType.MESH

QK = 256
NX, NY, NZL, NZH = 4, 8, 8, 2
NZ = NZL * NZH
REACH = 4
TOK = 384
CHUNK = 256
HALF = 128
FULL = 512
COLS = 12
BLOCKS = NX * NZH * 2
ROWS_A = NY * NZL * 8
ROWS_B = NZL * NY * 4
ROWS_G = 16

VMEM_ALL = 67_043_328

beta_first = 0.9
beta_second = 0.999
learn_rate = 0.001
adam_eps = 1e-08
fix_first = 1.0 - (0.9**10) ** 10
fix_second = 1.0 - (0.999**10) ** 10

NT = (((1,), (1,)), ((), ()))


def adam(master, first, second, gradient):
    new_first = beta_first * first + (1.0 - beta_first) * gradient
    new_second = beta_second * second + (1.0 - beta_second) * gradient * gradient
    new_master = master - learn_rate * (new_first / fix_first) / (
        jnp.sqrt(new_second / fix_second) + adam_eps
    )
    return new_master, new_first, new_second


def gather_kernel(
    tokens,
    master,
    first,
    second,
    gradient,
    gate,
    out,
    gate_out,
    state,
    gate_in,
    x,
    pa,
    y1,
    pb,
    pg,
    gate_far,
    wt,
    a_rows,
    b_rows,
    g_rows,
    a_give,
    b_give,
    g_give,
    send_sem,
    recv_sem,
    local_sem,
):
    group, inner = lax.axis_index("group"), lax.axis_index("inner")
    zl, y = group // NY, group % NY
    xc, zh, core = inner // 4, (inner // 2) % 2, inner % 2
    z = zh * NZL + zl
    here = (xc, zh, y, zl)

    def device(x_=xc, y_=y, z_=z, core_=core):
        return ((z_ % NZL) * NY + y_, x_ * 4 + (z_ // NZL) * 2 + core_)

    def at_x(r):
        return device(x_=(xc + r + NX) % NX)

    def at_y(r):
        return device(y_=(y + r + NY) % NY)

    def at_z(r):
        return device(z_=(z + r + NZ) % NZ)

    other = device(core_=1 - core)

    loads = [
        pltpu.make_async_copy(src, dst, local_sem.at[1 + k])
        for k, (src, dst) in enumerate(
            [(ref, state.at[k]) for k, ref in enumerate((master, first, second, gradient))]
            + [(gate, gate_in)]
        )
    ]
    for c in loads:
        c.start()
    own_tokens = pltpu.make_async_copy(tokens, x.at[pl.ds(TOK, TOK)], local_sem.at[0])
    own_tokens.start()

    barrier = pltpu.get_barrier_semaphore()
    peers = (
        [at_z(sign * r) for r in range(1, REACH + 1) for sign in (1, -1)]
        + [at_y(r) for r in range(1, NY)]
        + [at_x(r) for r in range(1, NX)]
        + [other]
    )
    for peer in peers:
        pl.semaphore_signal(barrier, inc=1, device_id=peer, device_id_type=MESH)

    for c in loads:
        c.wait()
    new_master, _, _ = adam(state[0], state[1], state[2], state[3])
    pa[(0, *here, core)] = new_master[0:8, 0:HALF].astype(jnp.bfloat16)
    pa[(1, *here, core)] = new_master[0:8, HALF:].astype(jnp.bfloat16)
    y1[y, core] = jnp.concatenate(
        [new_master[8:12, 0:HALF], new_master[8:12, HALF:]], axis=0
    ).astype(jnp.bfloat16)
    gate_rows = jnp.concatenate(
        [gate_in[...].astype(jnp.float32), jnp.zeros((ROWS_G - 2, CHUNK), jnp.float32)], axis=0
    ).astype(jnp.bfloat16)
    pg[xc, core, 0] = gate_rows[:, 0:HALF]
    pg[xc, core, 1] = gate_rows[:, HALF:]

    pl.semaphore_wait(barrier, len(peers))

    a_tiles = (pa.at[(slice(0, 2), *here, 1)],) * 2
    b_tile = (y1.at[y, 0],) * 2
    g_tile = (pg.at[xc, 0],) * 2
    all_tokens = (tokens, x.at[pl.ds(0, TOK)])
    a_parts = [
        (a_give.at[pl.ds(k * 32, 32)], a_rows.at[pl.ds(k * 32, 32)]) for k in range(2)
    ]
    b_part, g_part = (b_give, b_rows), (g_give, g_rows)
    across = [a_tiles, b_tile, g_tile, all_tokens, *a_parts, b_part, g_part]

    def cross(pair):
        k = [p is pair for p in across].index(True)
        return pltpu.make_async_remote_copy(
            src_ref=pair[0],
            dst_ref=pair[1],
            send_sem=send_sem.at[k],
            recv_sem=recv_sem.at[k],
            device_id=other,
            device_id_type=MESH,
        )

    class Plan:
        def __init__(self):
            self.used, self.started = len(across), []

        def go(self, src, dev, dst=None):
            k = self.used
            self.used += 1
            c = pltpu.make_async_remote_copy(
                src_ref=src,
                dst_ref=src if dst is None else dst,
                send_sem=send_sem.at[k],
                recv_sem=recv_sem.at[k],
                device_id=dev,
                device_id_type=MESH,
            )
            c.start()
            self.started.append(c)
            return c

        def give(self, pair):
            c = cross(pair)
            c.start()
            self.started.append(c)

    def ring(go, count, chunks, region, coord, neighbour, landed):
        half = count // 2
        copies = {}

        def begin(parts):
            for k in parts:
                for sign in (1, -1):
                    copies[sign, 1, k] = go(region(coord, k), neighbour(sign))
            for k in parts:
                landed(coord, k)

        def advance(step, k):
            blocks = []
            for sign in (1, -1):
                if (sign, step, k) in copies:
                    copies[sign, step, k].wait_recv()
                    last = step + 1 == half
                    block = (coord - sign * step + count) % count
                    blocks.append(block)
                    if step < half and (not last or (k < chunks // 2) == (sign > 0)):
                        copies[sign, step + 1, k] = go(region(block, k), neighbour(sign))
            for block in blocks:
                landed(block, k)

        return begin, advance

    def run(events):
        for _, event in sorted(events, key=lambda e: e[0]):
            event()

    @pl.when(core == 0)
    def _():
        plan = Plan()
        go = plan.go
        plan.give(b_tile)
        plan.give(g_tile)
        cross(a_tiles).wait_recv()

        def tile(slots, block):
            return pa.at[slots, xc, block // NZL, y, block % NZL]

        both = slice(0, 2)
        along_x, along_y = [], []

        def spread_x(block):
            along_x.extend(go(tile(0, block), at_x(r)) for r in (2, 1, 3))

        def spread_y(block):
            along_y.extend(go(tile(1, block), at_y(r)) for r in (4, 3, 5, 2, 6, 1, 7))

        a_z = {}
        for r in range(REACH, 0, -1):
            for sign in (1, -1):
                a_z[sign, r] = go(tile(both, z), at_z(sign * r))
        spread_y(z)
        spread_x(z)
        plan.give(all_tokens)
        for r in range(1, 2 * REACH + 1):
            for sign in (1, -1):
                block = (z - sign * r + NZ) % NZ
                a_z[sign, r].wait_recv()
                if r <= REACH:
                    slots = both if r < REACH else slice(0, 1) if sign > 0 else slice(1, 2)
                    a_z[sign, REACH + r] = go(tile(slots, block), at_z(sign * REACH))
                if r < 2 * REACH or sign < 0:
                    spread_y(block)
                if r < 2 * REACH or sign > 0:
                    spread_x(block)

        def landed_y(b, k):
            rows = pl.ds(pl.multiple_of(b * 64, 64), 64)
            for far in range(NZH):
                for parity in range(2):
                    lanes = pl.ds((4 * k + 2 * far + parity) * CHUNK, HALF)
                    wt[rows, lanes] = pa[0, k, far, b, :, parity].reshape(64, HALF)

        def landed_x(b, k):
            far, top = k // 4, 2 * (k % 4)
            for parity in range(2):
                lane = pl.multiple_of((4 * b + 2 * far + parity) * CHUNK + HALF, HALF)
                wt[top * 64 : top * 64 + 128, pl.ds(lane, HALF)] = jnp.concatenate(
                    [pa[1, b, far, top + n, :, parity].reshape(64, HALF) for n in range(2)], axis=0
                )

        y_begin, y_step = ring(
            go, NY, NX, lambda b, k: pa.at[0, k, :, b], y, at_y, landed_y
        )
        x_begin, x_step = ring(
            go,
            NX,
            8,
            lambda b, k: pa.at[1, b, k // 4, pl.ds(2 * (k % 4), 2)],
            xc,
            at_x,
            landed_x,
        )

        def start(copies, begin, chunks):
            for c in copies:
                c.wait_recv()
            begin(range(chunks))

        events = [
            (13.6, lambda: start(along_x, y_begin, NX)),
            (15.6, lambda: start(along_y, x_begin, 8)),
        ]
        for step in range(1, NY // 2 + 1):
            for k in range(NX):
                events.append((16.3 + 2.8 * (step - 1) + 0.7 * k, functools.partial(y_step, step, k)))
        for step in range(1, NX // 2 + 1):
            for k in range(8):
                when = 18.5 + 5.6 * (step - 1) + 0.7 * (k if step == 1 else k % 4)
                events.append((when, functools.partial(x_step, step, k)))
        run(events)

        own_tokens.wait()
        cross(all_tokens).wait_recv()
        for k in range(2):
            res = lax.dot_general(
                wt[k * 256 : (k + 1) * 256], x[0:FULL], NT, preferred_element_type=jnp.float32
            )
            res = res.reshape(32, 8, FULL).astype(jnp.bfloat16)
            a_give[k * 32 : (k + 1) * 32] = res[:, :, :TOK]
            plan.give(a_parts[k])
            a_rows[k * 32 : (k + 1) * 32, :, 0 : FULL - TOK] = res[:, :, TOK:]
        for k in range(2):
            res = lax.dot_general(
                wt[k * 256 : (k + 1) * 256], x[FULL:], NT, preferred_element_type=jnp.float32
            )
            a_rows[k * 32 : (k + 1) * 32, :, FULL - TOK :] = res.reshape(
                32, 8, 2 * TOK - FULL
            ).astype(jnp.bfloat16)
        cross(g_part).wait_recv()
        cross(b_part).wait_recv()
        for c in plan.started:
            c.wait_send()

    @pl.when(core == 1)
    def _():
        plan = Plan()
        go = plan.go
        plan.give(a_tiles)
        cross(b_tile).wait_recv()
        b_y = [go(y1.at[y], at_y(r)) for r in (4, 3, 5, 2, 6, 1, 7)]
        cross(g_tile).wait_recv()
        g_x = [go(pg.at[xc], at_x(r)) for r in (2, 1, 3)]
        plan.give(all_tokens)
        for c in b_y:
            c.wait_recv()
        upper = lax.broadcasted_iota(jnp.int32, (8, HALF), 0) < 4
        for parity in range(2):
            low, high = [], []
            for a in range(NY // 2):
                even = y1[2 * a, parity].astype(jnp.float32)
                odd = y1[2 * a + 1, parity].astype(jnp.float32)
                low.append(jnp.where(upper, even, pltpu.roll(odd, 4, 0)))
                high.append(jnp.where(upper, pltpu.roll(even, 4, 0), odd))
            pb[xc, zh, zl, parity, 0] = jnp.concatenate(low, axis=0).astype(jnp.bfloat16)
            pb[xc, zh, zl, parity, 1] = jnp.concatenate(high, axis=0).astype(jnp.bfloat16)
        for c in g_x:
            c.wait_recv()
        b_x = [go(pb.at[xc, zh, zl], at_x(r)) for r in (1, 3, 2)]

        def landed_z(b, k):
            mx, far, low_z = (xc + k) % NX, b // NZL, b % NZL
            rows = pl.ds(pl.multiple_of(low_z * 32, 32), 32)
            for parity in range(2):
                for kh in range(2):
                    lane = (4 * mx + 2 * far + parity) * CHUNK + kh * HALF
                    wt[rows, pl.ds(pl.multiple_of(lane, HALF), HALF)] = pb[
                        mx, far, low_z, parity, kh
                    ]

        begin, step_of = ring(
            go,
            NZ,
            NX,
            lambda b, k: pb.at[(xc + k) % NX, b // NZL, b % NZL],
            z,
            at_z,
            landed_z,
        )
        begin((0,))
        g_z = [
            go(pg, at_z(sign * REACH), gate_far.at[k]) for k, sign in ((0, 1), (1, -1))
        ]

        def start(c, k):
            c.wait_recv()
            begin((k,))

        events = [
            (2.5, lambda: start(b_x[0], 3)),
            (2.6, lambda: start(b_x[1], 1)),
            (3.6, lambda: start(b_x[2], 2)),
        ]
        for step in range(1, NZ // 2 + 1):
            for k, late in ((0, 0.3), (1, 2.9), (3, 3.2), (2, 4.2)):
                events.append((late + 2.4 * step, functools.partial(step_of, step, k)))
        run(events)

        for c in g_z:
            c.wait_recv()
        for mx in range(NX):
            for parity in range(2):
                for kh in range(2):
                    near = (4 * mx + 2 * zh + parity) * CHUNK + kh * HALF
                    far = (4 * mx + 2 * (1 - zh) + parity) * CHUNK + kh * HALF
                    rows = pl.ds(ROWS_B, ROWS_G)
                    wt[rows, pl.ds(pl.multiple_of(near, HALF), HALF)] = pg[mx, parity, kh]
                    wt[rows, pl.ds(pl.multiple_of(far, HALF), HALF)] = gate_far[
                        zl // REACH, mx, parity, kh
                    ]
        own_tokens.wait()
        cross(all_tokens).wait_recv()
        res = lax.dot_general(
            wt[0 : ROWS_B + ROWS_G], x[0:FULL], NT, preferred_element_type=jnp.float32
        )
        rows = res[:ROWS_B].reshape(32, 8, FULL).astype(jnp.bfloat16)
        b_give[...] = rows[:, :, :TOK]
        plan.give(b_part)
        g_give[...] = res[ROWS_B:, :TOK]
        plan.give(g_part)
        b_rows[:, :, 0 : FULL - TOK] = rows[:, :, TOK:]
        g_rows[:, 0 : FULL - TOK] = res[ROWS_B:, TOK:]
        res = lax.dot_general(
            wt[0 : ROWS_B + ROWS_G], x[FULL:], NT, preferred_element_type=jnp.float32
        )
        b_rows[:, :, FULL - TOK :] = (
            res[:ROWS_B].reshape(32, 8, 2 * TOK - FULL).astype(jnp.bfloat16)
        )
        g_rows[:, FULL - TOK :] = res[ROWS_B:]
        for pair in a_parts:
            cross(pair).wait_recv()
        for c in plan.started:
            c.wait_send()

    gate_out[...] = g_rows[0:8]
    first4 = lax.broadcasted_iota(jnp.int32, (8, TOK), 0) < 4
    for l in range(NZL):
        rows = []
        for a in range(NY // 2):
            t0 = a_rows[2 * a * NZL + l].astype(jnp.float32)
            a1 = a_rows[(2 * a + 1) * NZL + l].astype(jnp.float32)
            b = b_rows[l * (NY // 2) + a].astype(jnp.float32)
            turned = pltpu.roll(a1, 4, 0)
            rows += [t0, jnp.where(first4, b, turned), jnp.where(first4, turned, b)]
        out[l * 96 : l * 96 + 96] = jnp.concatenate(rows, axis=0).astype(jnp.bfloat16)


def head_kernel(
    projected,
    gates,
    input_bias,
    forget_bias,
    master,
    first,
    second,
    gradient,
    new_master,
    new_first,
    new_second,
    hidden,
    state,
    updated,
    sems,
):
    loads = [
        pltpu.make_async_copy(ref, state.at[k], sems.at[k])
        for k, ref in enumerate((master, first, second, gradient))
    ]
    for c in loads:
        c.start()
    for c in loads:
        c.wait()
    updated[0], updated[1], updated[2] = adam(state[0], state[1], state[2], state[3])
    stores = [
        pltpu.make_async_copy(updated.at[k], ref, sems.at[4 + k])
        for k, ref in enumerate((new_master, new_first, new_second))
    ]
    for c in stores:
        c.start()
    pre = gates[...]
    input_gate = pre[0:1] + input_bias[0]
    forget = pre[1:2] + forget_bias[0]
    forget_log = jnp.minimum(forget, 0.0) - jnp.log1p(jnp.exp(-jnp.abs(forget)))
    t = lax.broadcasted_iota(jnp.int32, (TOK, TOK), 0)
    s = lax.broadcasted_iota(jnp.int32, (TOK, TOK), 1)
    causal = t >= s
    column = jnp.sum(jnp.where(causal, forget_log, 0.0), axis=1, keepdims=True)
    lane = lax.broadcasted_iota(jnp.int32, (8, TOK), 1)
    scan = jnp.broadcast_to(forget_log, (8, TOK))
    step = 1
    while step < TOK:
        scan = scan + jnp.where(lane >= step, pltpu.roll(scan, step, 1), 0.0)
        step *= 2
    row = scan[0:1]
    decay = jnp.exp(jnp.where(causal, column - row + input_gate, -jnp.inf))
    query = projected[0:QK].T
    scores = jnp.dot(query, projected[QK : 2 * QK], preferred_element_type=jnp.float32)
    weighted = scores * QK ** (-0.5) * decay
    normalizer = jnp.sum(weighted, axis=1, keepdims=True)
    numerator = lax.dot_general(
        weighted.astype(jnp.bfloat16),
        projected[2 * QK :],
        NT,
        preferred_element_type=jnp.float32,
    )
    hidden[...] = (numerator / jnp.maximum(jnp.abs(normalizer), 1.0)).astype(jnp.bfloat16)
    for c in stores:
        c.wait()


def on_device(
    tokens,
    master_weight,
    first_moment,
    second_moment,
    gradient,
    gate_weight,
    input_bias,
    forget_bias,
):
    state = [a.T for a in (master_weight, first_moment, second_moment, gradient)]
    vmem = pl.BlockSpec(memory_space=pltpu.VMEM)
    smem = pl.BlockSpec(memory_space=pltpu.SMEM)
    hbm = pl.BlockSpec(memory_space=pltpu.HBM)
    bf16, f32 = jnp.bfloat16, jnp.float32
    copies = 256
    projected, gates = pl.pallas_call(
        gather_kernel,
        out_shape=(
            jax.ShapeDtypeStruct((3 * QK, TOK), bf16),
            jax.ShapeDtypeStruct((8, TOK), f32),
        ),
        in_specs=[hbm] * 6,
        out_specs=(vmem, vmem),
        scratch_shapes=[
            pltpu.VMEM((4, COLS, CHUNK), f32),
            pltpu.VMEM((2, CHUNK), bf16),
            pltpu.VMEM((2 * TOK, BLOCKS * CHUNK), bf16),
            pltpu.VMEM((2, NX, NZH, NY, NZL, 2, 8, HALF), bf16),
            pltpu.VMEM((NY, 2, 8, HALF), bf16),
            pltpu.VMEM((NX, NZH, NZL, 2, 2, 32, HALF), bf16),
            pltpu.VMEM((NX, 2, 2, ROWS_G, HALF), bf16),
            pltpu.VMEM((2, NX, 2, 2, ROWS_G, HALF), bf16),
            pltpu.VMEM((ROWS_A, BLOCKS * CHUNK), bf16),
            pltpu.VMEM((64, 8, TOK), bf16),
            pltpu.VMEM((32, 8, TOK), bf16),
            pltpu.VMEM((ROWS_G, TOK), f32),
            pltpu.VMEM((64, 8, TOK), bf16),
            pltpu.VMEM((32, 8, TOK), bf16),
            pltpu.VMEM((ROWS_G, TOK), f32),
            pltpu.SemaphoreType.DMA((copies,)),
            pltpu.SemaphoreType.DMA((copies,)),
            pltpu.SemaphoreType.DMA((6,)),
        ],
        compiler_params=pltpu.CompilerParams(
            collective_id=0, has_side_effects=True, vmem_limit_bytes=VMEM_ALL
        ),
        name="gather_project",
    )(tokens, *state, gate_weight.T)
    new_master, new_first, new_second, hidden = pl.pallas_call(
        head_kernel,
        out_shape=tuple(jax.ShapeDtypeStruct((COLS, CHUNK), f32) for _ in range(3))
        + (jax.ShapeDtypeStruct((TOK, QK), bf16),),
        in_specs=[vmem, vmem, smem, smem] + [hbm] * 4,
        out_specs=(hbm,) * 3 + (vmem,),
        scratch_shapes=[
            pltpu.VMEM((4, COLS, CHUNK), f32),
            pltpu.VMEM((3, COLS, CHUNK), f32),
            pltpu.SemaphoreType.DMA((7,)),
        ],
        compiler_params=pltpu.CompilerParams(vmem_limit_bytes=VMEM_ALL),
        name="head",
    )(projected, gates, input_bias, forget_bias, *state)
    return new_master.T, new_first.T, new_second.T, hidden


def solution(mesh):
    placed = (
        P(("group", "inner"), None),
        P("inner", "group"),
        P("inner", "group"),
        P("inner", "group"),
        P("inner", "group"),
        P("inner", None),
        P(),
        P(),
    )
    return jax.shard_map(
        on_device,
        mesh=mesh,
        in_specs=placed,
        out_specs=(
            P("inner", "group"),
            P("inner", "group"),
            P("inner", "group"),
            P(("group", "inner"), None),
        ),
        check_vma=False,
    )
```
